1024 devices in a mesh: expert: 16 (over z_hi, y, core), dp: 64 (over x, z_lo).
Axes of the slice: x: 4, y: 4, z: 32 (z_hi: 2, z_lo: 16; z = z_hi * 16 + z_lo), core: 2. Of those that a mesh axis runs over, the one named last changes fastest.
Arguments:
- tokens: bfloat16 [131072, 2048], P(('expert', 'dp')), may hold values from -6 to 6
- out_grad: bfloat16 [131072, 2048], P(('expert', 'dp')), may hold values from -6 to 6
- expert_ids: int32 [131072, 1], P(('expert', 'dp')), may hold values from 0 to 15; in each aligned block of 128 rows (0 to 127, 128 to 255, ...) at most 12 rows name the same one
- combine_ints: int32 [131072, 8], P(('expert', 'dp')), may hold values from 1 to 15
- w_gate: bfloat16 [16, 2048, 384], P('expert'), may hold values from -0.125 to 0.125
- w_up: bfloat16 [16, 2048, 384], P('expert'), may hold values from -0.125 to 0.125
- w_down: bfloat16 [16, 384, 2048], P('expert'), may hold values from -0.3125 to 0.3125
Outputs:
- combined: bfloat16 [131072, 2048], P(('expert', 'dp'))
- dinput: bfloat16 [131072, 2048], P(('expert', 'dp'))
- grad_down: float32 [16, 384, 2048], P('expert', None, 'dp')
The draws below stay inside these ranges and needn't reach their ends.
Inputs may be any that keep to these rules, and one draw needn't show every extreme that they name: `expert_ids`: each row names one expert of the window. Among the 128 rows of one device no expert is named more than 12 times, and in every draw some expert is named exactly 12 times by the rows of some device.
All inputs are finite; a program needn't handle non-finite values.
Results may differ from the reference program's by a relative error of at most 0.0057.
Values may be sent and summed in bfloat16 or wider, within the bound.
No kernel may reach another device: no remote copies, remote signals or barrier semaphores. Data moves between devices by JAX's collectives and lax.ppermute only.
A program may use at most 64 MiB of HBM per device.

```python
import math
import jax
import jax.numpy as jnp
import numpy as np
from jax import lax

D = 2048
FFW = 384
EXPERTS = 16
TOP = 8
ROUTES = 1
TOK_DEV = 128
CAP = 12
TOKENS = 131072


def set_ends(array, key, low, largest):
    index_at = [jax.random.randint(jax.random.fold_in(key, axis), (), 0, length) for axis, length in enumerate(array.shape)]
    longest = array.shape.index(max(array.shape))
    next_to = index_at[:longest] + [(index_at[longest] + 1) % array.shape[longest]] + index_at[longest + 1:]
    return array.at[tuple(index_at)].set(low).at[tuple(next_to)].set(largest)


def level_of(key, shape, cuts, smallest, high):
    def one(position, parts):
        draws = jax.random.uniform(jax.random.fold_in(jax.random.fold_in(key, 6), position), (parts,), jnp.float32, smallest / len(cuts), high / len(cuts))
        return jnp.repeat(jnp.exp(draws), shape[position] // parts).reshape((-1,) + (1,) * (len(shape) - position - 1))

    factor_of = one(*cuts[0])
    for cut in cuts[1:]:
        factor_of = factor_of * one(*cut)
    return factor_of


def shared_out(rng, own, number, rows, count, top, limit, skew):
    ranking = jax.random.permutation(rng, count)
    crowded, common = portions_of(count, rows * top, limit, skew, True), portions_of(count, rows * top, limit, skew, False)
    places = jnp.arange(count)

    def named(sizes, rotation):
        used = int((sizes > 0).sum())
        fixed = max(1, used // 4)
        passed = fixed + (places - fixed + rotation * (used - fixed)) % max(1, count - fixed)
        return jnp.zeros((count,), jnp.int32).at[ranking[jnp.where(places < fixed, places, passed)]].set(jnp.asarray(sizes, jnp.int32))

    sizes = jnp.where(number % 4 == 0, named(crowded, number // 4), named(common, number - number // 4 - 1))
    mixed = jax.random.permutation(jax.random.fold_in(own, 3), count)
    source_of, receiver = mixed[0:count // 2 * 2:2], mixed[1:count // 2 * 2:2]
    margin = jnp.minimum(sizes[source_of] - 1, limit - sizes[receiver]) // 2
    margin = jnp.where((source_of == ranking[0]) | (receiver == ranking[0]) | (sizes[receiver] == 0), 0, jnp.maximum(margin, 0))
    passed = jax.random.randint(jax.random.fold_in(own, 4), (count // 2,), 0, 1 << 20) % (margin + 1)
    sizes = sizes.at[source_of].add(-passed).at[receiver].add(passed)
    labels = jnp.searchsorted(jnp.cumsum(sizes), jnp.arange(rows * top), side="right").astype(jnp.int32)
    table = labels.reshape(top, rows).T
    table = table[jax.random.permutation(jax.random.fold_in(own, 1), rows)]
    rotation = jax.random.randint(jax.random.fold_in(own, 2), (rows, 1), 0, top)
    return jnp.take_along_axis(table, (jnp.arange(top)[None, :] + rotation) % top, axis=1)


def portions_of(count, total, most, skew, full):
    portions = [(1 << 20) // math.isqrt(rank ** skew) + 1 for rank in range(1, count + 1)]
    largest = most if full else min(most, max(-(-total // count), total * portions[0] // sum(portions)))
    least = 1 if total - largest >= count - 1 else 0
    counts, spare = [largest] + [least] * (count - 1), total - largest - least * (count - 1)
    while spare > 0:
        free = [i for i in range(1, count) if counts[i] < largest] or [i for i in range(1, count) if counts[i] < most]
        pool, left = sum([portions[i] for i in free]), spare
        for i in free:
            extra = min(most - counts[i], max(1, left * portions[i] // pool), spare)
            counts[i] = counts[i] + extra
            spare = spare - extra
    return np.array(counts)


def bell_draw(stream_key, shape, deviation, bound, split=(), kind=jnp.bfloat16):
    values = jax.random.normal(stream_key, shape, jnp.float32) * deviation
    if len(split) > 0:
        values = level_of(stream_key, shape, split, -0.22, 0.18) * values
    return jnp.clip(values, min=-bound, max=bound).astype(kind)


def setup_inputs(seed: int = 0) -> dict:
    key_list = jax.random.split(jax.random.key(seed), 8)
    tokens = bell_draw(key_list[0], (TOKENS, D), 1.0, 6.0, ((0, 1024),))
    out_grad = bell_draw(key_list[1], (TOKENS, D), 1.0, 6.0, ((0, 1024),))
    expert_ids_keys = jax.random.split(jax.random.fold_in(key_list[2], 1), TOKENS // TOK_DEV)
    expert_ids_turns = jax.random.permutation(jax.random.fold_in(key_list[2], 3), TOKENS // TOK_DEV)
    expert_ids = jax.vmap(lambda own, number: shared_out(jax.random.fold_in(key_list[2], 2), own, number, TOK_DEV, EXPERTS, ROUTES, CAP, 2))(expert_ids_keys, expert_ids_turns).reshape((TOKENS, ROUTES))
    combine_ints = set_ends(jax.random.randint(key_list[3], (TOKENS, TOP), 1, 16), jax.random.fold_in(key_list[3], 1), 1, 15).astype(jnp.int32)
    w_gate = bell_draw(key_list[4], (EXPERTS, D, FFW), D ** -0.5, 0.125, ((0, 16),))
    w_up = bell_draw(key_list[5], (EXPERTS, D, FFW), D ** -0.5, 0.125, ((0, 16),))
    w_down = bell_draw(key_list[6], (EXPERTS, FFW, D), FFW ** -0.5, 0.3125, ((0, 16),))
    return {"tokens": tokens, "out_grad": out_grad, "expert_ids": expert_ids, "combine_ints": combine_ints, "w_gate": w_gate, "w_up": w_up, "w_down": w_down}


def reference(tokens, out_grad, expert_ids, combine_ints, w_gate, w_up, w_down):
    sources = TOKENS // TOK_DEV
    buf_rows = sources * CAP
    flat_ids = expert_ids.reshape(sources, TOK_DEV * ROUTES)
    onehot = (flat_ids[:, :, None] == jnp.arange(EXPERTS, dtype=jnp.int32)[None, None, :]).astype(jnp.int32)
    slot_rank = jnp.sum((jnp.cumsum(onehot, axis=1) - onehot) * onehot, axis=2).reshape(TOKENS, ROUTES)
    block_base = (jnp.arange(TOKENS, dtype=jnp.int32) // TOK_DEV) * CAP
    all_weights = combine_ints.astype(jnp.float32)
    weights = all_weights[:, :ROUTES] / jnp.sum(all_weights, axis=1, keepdims=True)
    grad_full = out_grad.astype(jnp.float32)

    def per_expert(totals, inputs):
        out_sum, grad_sum = totals
        expert, gate_mat, up_mat, down_mat = inputs
        routed = expert_ids == expert
        slot_pos = jnp.where(routed, block_base[:, None] + slot_rank, buf_rows).astype(jnp.int32)
        row_buf = jnp.zeros((buf_rows, D), jnp.bfloat16)
        grad_buf = jnp.zeros((buf_rows, D), jnp.bfloat16)
        for route_k in range(ROUTES):
            row_buf = row_buf.at[slot_pos[:, route_k]].set(tokens, mode="drop")
            scaled = (weights[:, route_k:route_k + 1] * grad_full).astype(jnp.bfloat16)
            grad_buf = grad_buf.at[slot_pos[:, route_k]].set(scaled, mode="drop")
        gate_act = jnp.dot(row_buf, gate_mat, preferred_element_type=jnp.float32)
        up_act = jnp.dot(row_buf, up_mat, preferred_element_type=jnp.float32)
        gate_sig = jax.nn.sigmoid(gate_act)
        gate_silu = gate_act * gate_sig
        hidden = (gate_silu * up_act).astype(jnp.bfloat16)
        result = jnp.dot(hidden, down_mat, preferred_element_type=jnp.float32).astype(jnp.bfloat16)
        dhidden = jnp.dot(grad_buf, down_mat.T, preferred_element_type=jnp.float32)
        grad_gate = (dhidden * up_act * gate_sig * (1.0 + gate_act * (1.0 - gate_sig))).astype(jnp.bfloat16)
        grad_up = (dhidden * gate_silu).astype(jnp.bfloat16)
        slot_grad = (jnp.dot(grad_gate, gate_mat.T, preferred_element_type=jnp.float32)
                     + jnp.dot(grad_up, up_mat.T, preferred_element_type=jnp.float32)).astype(jnp.bfloat16)
        grad_mat = jnp.dot(hidden.T, grad_buf, preferred_element_type=jnp.float32)
        clipped = jnp.minimum(slot_pos, buf_rows - 1)
        for route_k in range(ROUTES):
            picked = routed[:, route_k:route_k + 1]
            out_sum = out_sum + jnp.where(picked, weights[:, route_k:route_k + 1] * result[clipped[:, route_k]].astype(jnp.float32), jnp.float32(0.0))
            grad_sum = grad_sum + jnp.where(picked, slot_grad[clipped[:, route_k]].astype(jnp.float32), jnp.float32(0.0))
        return (out_sum, grad_sum), grad_mat

    start_sums = (jnp.zeros((TOKENS, D), jnp.float32), jnp.zeros((TOKENS, D), jnp.float32))
    (out_sum, grad_sum), grad_down = lax.scan(per_expert, start_sums, (jnp.arange(EXPERTS, dtype=jnp.int32), w_gate, w_up, w_down))
    return out_sum.astype(jnp.bfloat16), grad_sum.astype(jnp.bfloat16), grad_down
```

```python
import functools

import jax
import jax.numpy as jnp
from jax import lax
from jax.experimental import pallas as pl
from jax.experimental.pallas import tpu as pltpu
from jax.sharding import Mesh, PartitionSpec as P

CAP = 12
AXES = ("zh", "y", "c", "x", "zl")
SPLIT = (2, 4, 2, 4, 16)
BF16 = jnp.bfloat16
F32 = jnp.float32


def dot(a, b, ca=1, cb=0):
    return lax.dot_general(a, b, (((ca,), (cb,)), ((), ())), preferred_element_type=F32)


def slot_onehot(ids, near, halves):
    tokens = ids.shape[1]
    experts = near * halves
    hot = (lax.broadcasted_iota(jnp.int32, (experts, tokens), 0) == ids).astype(F32)
    before = (
        lax.broadcasted_iota(jnp.int32, (tokens, tokens), 0)
        < lax.broadcasted_iota(jnp.int32, (tokens, tokens), 1)
    ).astype(BF16)
    counts = dot(hot.astype(BF16), before)
    rank = jnp.sum(hot * counts, axis=0, keepdims=True).astype(jnp.int32)
    half = sum((ids >= near * k).astype(jnp.int32) for k in range(1, halves))
    slot = (ids - near * half) * (halves * CAP) + half * CAP + rank
    return lax.broadcasted_iota(jnp.int32, (experts * CAP, tokens), 0) == slot


def token_weights(ints):
    ints = ints.astype(F32)
    return ints[0:1] / jnp.sum(ints, axis=0, keepdims=True)


def dispatch_kernel(near, halves, ids_ref, ints_ref, tok_ref, grad_ref, rows_ref, grads_ref):
    hot = slot_onehot(ids_ref[...], near, halves)
    pick = hot.astype(BF16)
    rows_ref[...] = dot(pick, tok_ref[...]).astype(BF16)
    scale = jnp.sum(jnp.where(hot, token_weights(ints_ref[...]), 0.0), axis=1, keepdims=True)
    grads_ref[...] = (scale * dot(pick, grad_ref[...])).astype(BF16)


def combine_kernel(near, halves, ids_ref, ints_ref, rows_ref, grads_ref, out_ref, din_ref):
    hot = slot_onehot(ids_ref[...], near, halves)
    pick = hot.astype(BF16)
    tokens = pick.shape[1]
    eye = lax.broadcasted_iota(jnp.int32, (tokens, tokens), 0) == lax.broadcasted_iota(
        jnp.int32, (tokens, tokens), 1
    )
    scale = jnp.sum(jnp.where(eye, token_weights(ints_ref[...]), 0.0), axis=1, keepdims=True)
    out_ref[...] = (scale * dot(pick, rows_ref[...], 0, 0)).astype(BF16)
    din_ref[...] = dot(pick, grads_ref[...], 0, 0).astype(BF16)


def pieces_kernel(at_ref, gate_ref, up_ref, down_ref, out_ref):
    rows = gate_ref.shape[0]
    lanes = down_ref.shape[1]
    shift = lax.rem(at_ref[0], lanes // rows) * rows
    pick = (
        lax.broadcasted_iota(jnp.int32, (rows, lanes), 1)
        == lax.broadcasted_iota(jnp.int32, (rows, lanes), 0) + shift
    ).astype(BF16)
    out_ref[0] = gate_ref[...]
    out_ref[1] = up_ref[...]
    out_ref[2] = dot(pick, down_ref[...], 1, 1).astype(BF16)


def expert_math(rows, grads, keep, w_gate, w_up, dh):
    gate = dot(rows, w_gate)
    up = dot(rows, w_up)
    sig = jax.nn.sigmoid(gate)
    silu = gate * sig
    zero = jnp.zeros_like(gate)
    hidden = jnp.where(keep, silu * up, zero).astype(BF16)
    dgate = jnp.where(keep, dh * up * sig * (1.0 + gate * (1.0 - sig)), zero).astype(BF16)
    dup = jnp.where(keep, dh * silu, zero).astype(BF16)
    return hidden, dgate, dup


def row_mask(half, count, halves, width):
    at = lax.broadcasted_iota(jnp.int32, (count, width), 0)
    return lax.div(lax.rem(at, halves * CAP), CAP) == half


def near_kernel(halves, half_ref, rows_ref, grads_ref, wg_ref, wu_ref, wd_ref, out_ref, dx_ref, gt_ref):
    rows, grads = rows_ref[...], grads_ref[...]
    w_gate, w_up, w_down = wg_ref[...], wu_ref[...], wd_ref[...]
    keep = row_mask(half_ref[0], rows.shape[0], halves, w_gate.shape[1])
    hidden, dgate, dup = expert_math(rows, grads, keep, w_gate, w_up, dot(grads, w_down, 1, 1))
    out_ref[...] = dot(hidden, w_down).astype(BF16)
    dx_ref[...] = (dot(dgate, w_gate, 1, 1) + dot(dup, w_up, 1, 1)).astype(BF16)
    gt_ref[...] = dot(grads, hidden, 0, 0)


def far_kernel(halves, half_ref, rows_ref, grads_ref, w_ref, o_ref, d_ref, out_ref, dx_ref, gt_ref):
    rows, grads = rows_ref[...], grads_ref[...]
    blocks, _, depth, width = w_ref.shape
    w_gate, w_up, w_down = (w_ref[:, k].reshape(blocks * depth, width) for k in range(3))
    keep = row_mask(1 - half_ref[0], rows.shape[0], halves, width)
    hidden, dgate, dup = expert_math(rows, grads, keep, w_gate, w_up, dot(grads, w_down))
    gt_ref[...] = dot(grads, hidden, 0, 0)
    out_ref[...] = dot(hidden, w_down, 1, 1).astype(BF16) + o_ref[...]
    dx_ref[...] = (dot(dgate, w_gate, 1, 1) + dot(dup, w_up, 1, 1)).astype(BF16) + d_ref[...]


def call(kernel, outs, *args, scalar=False, flops=0):
    vmem = pl.BlockSpec(memory_space=pltpu.VMEM)
    smem = pl.BlockSpec(memory_space=pltpu.SMEM)
    size = sum(a.size * a.dtype.itemsize for a in (*args, *outs))
    return pl.pallas_call(
        kernel,
        out_shape=outs,
        in_specs=[smem if scalar and k == 0 else vmem for k in range(len(args))],
        out_specs=tuple(vmem for _ in outs),
        compiler_params=pltpu.CompilerParams(vmem_limit_bytes=60 << 20),
        cost_estimate=pl.CostEstimate(flops=flops, bytes_accessed=size, transcendentals=0),
    )(*args)


def body(tokens, out_grad, expert_ids, combine_ints, w_gate, w_up, w_down):
    count, width = tokens.shape
    hidden_width = w_gate.shape[2]
    halves = lax.axis_size("zh")
    near = lax.axis_size("y") * lax.axis_size("c")
    nx, nz = lax.axis_size("x"), lax.axis_size("zl")
    shards = nx * nz
    depth = width // shards
    slots = near * halves * CAP
    half = lax.axis_index("zh").astype(jnp.int32).reshape(1)
    shard = (lax.axis_index("x") * nz + lax.axis_index("zl")).astype(jnp.int32).reshape(1)
    w_gate, w_up, w_down = w_gate[0], w_up[0], w_down[0]

    per = 128 // depth
    piece = pl.pallas_call(
        pieces_kernel,
        grid_spec=pltpu.PrefetchScalarGridSpec(
            num_scalar_prefetch=1,
            grid=(1,),
            in_specs=[
                pl.BlockSpec((depth, hidden_width), lambda i, at: (at[0], 0)),
                pl.BlockSpec((depth, hidden_width), lambda i, at: (at[0], 0)),
                pl.BlockSpec((hidden_width, 128), lambda i, at: (0, lax.div(at[0], per))),
            ],
            out_specs=pl.BlockSpec((3, depth, hidden_width), lambda i, at: (0, 0, 0)),
        ),
        out_shape=jax.ShapeDtypeStruct((3, depth, hidden_width), BF16),
    )(shard, w_gate, w_up, w_down)
    ring = lax.all_gather(
        piece.reshape(3 * depth, hidden_width), ("zh", "zl"), axis=0, tiled=True
    )
    other = lax.dynamic_slice_in_dim(
        ring, (1 - half[0]) * (nz * 3 * depth), nz * 3 * depth, axis=0
    )
    far = lax.all_gather(other, "x", axis=0, tiled=True).reshape(
        shards, 3, depth, hidden_width
    )

    ids = expert_ids.reshape(1, count)
    ints = combine_ints.T
    rows_shape = jax.ShapeDtypeStruct((slots, width), BF16)
    grad_shape = jax.ShapeDtypeStruct((width, hidden_width), F32)
    send_rows, send_grads = call(
        functools.partial(dispatch_kernel, near, halves),
        (rows_shape, rows_shape), ids, ints, tokens, out_grad,
        flops=4 * slots * count * width,
    )

    def swap(v):
        return lax.all_to_all(v, ("y", "c"), split_axis=0, concat_axis=0, tiled=True)

    rows, grads = swap(send_rows), swap(send_grads)
    work = 14 * slots * width * hidden_width
    near_out, near_dx, near_gt = call(
        functools.partial(near_kernel, halves),
        (rows_shape, rows_shape, grad_shape), half, rows, grads, w_gate, w_up, w_down,
        scalar=True, flops=work,
    )
    out, dx, far_gt = call(
        functools.partial(far_kernel, halves),
        (rows_shape, rows_shape, grad_shape), half, rows, grads, far, near_out, near_dx,
        scalar=True, flops=work,
    )

    def over_x(v):
        return lax.psum_scatter(v, "x", scatter_dimension=0, tiled=True)

    near_gx, far_gx = over_x(near_gt), over_x(far_gt)
    low = jnp.where(half[0] == 0, near_gx, far_gx)
    high = jnp.where(half[0] == 0, far_gx, near_gx)
    both = jnp.concatenate([low, high], axis=0)
    grad = lax.psum_scatter(both, ("zh", "zl"), scatter_dimension=0, tiled=True)

    combined, dinput = call(
        functools.partial(combine_kernel, near, halves),
        (jax.ShapeDtypeStruct((count, width), BF16),) * 2, ids, ints, swap(out), swap(dx),
        flops=4 * slots * count * width,
    )
    return combined, dinput, grad.T[None]


def build(mesh, split):
    fine = Mesh(mesh.devices.reshape(split), AXES)
    token = P(AXES, None)
    expert = P(("zh", "y", "c"), None, None)
    return jax.shard_map(
        body,
        mesh=fine,
        in_specs=(token, token, token, token, expert, expert, expert),
        out_specs=(token, token, P(("zh", "y", "c"), None, ("x", "zl"))),
        check_vma=False,
    )


def solution(mesh):
    return build(mesh, SPLIT)
```

```python
import functools

import jax
import jax.numpy as jnp
from jax import lax
from jax.experimental import pallas as pl
from jax.experimental.pallas import tpu as pltpu
from jax.sharding import Mesh, PartitionSpec as P


CAP = 12
AXES = ("zh", "y", "c", "x", "a", "b")
SPLIT = (2, 4, 2, 4, 4, 4)
BF16 = jnp.bfloat16
F32 = jnp.float32


def dot(a, b, ca=1, cb=0):
    return lax.dot_general(a, b, (((ca,), (cb,)), ((), ())), preferred_element_type=F32)


def slot_onehot(ids, near, halves, me):
    tokens = ids.shape[1]
    experts = near * halves
    hot = (lax.broadcasted_iota(jnp.int32, (experts, tokens), 0) == ids).astype(F32)
    before = (
        lax.broadcasted_iota(jnp.int32, (tokens, tokens), 0)
        < lax.broadcasted_iota(jnp.int32, (tokens, tokens), 1)
    ).astype(BF16)
    counts = dot(hot.astype(BF16), before)
    rank = jnp.sum(hot * counts, axis=0, keepdims=True).astype(jnp.int32)
    half = sum((ids >= near * k).astype(jnp.int32) for k in range(1, halves))
    owner = ids - near * half
    hops = jnp.where(owner >= me, owner - me, owner - me + near)
    slot = hops * (halves * CAP) + half * CAP + rank
    return lax.broadcasted_iota(jnp.int32, (experts * CAP, tokens), 0) == slot


def token_weights(ints):
    ints = ints.astype(F32)
    return ints[0:1] / jnp.sum(ints, axis=0, keepdims=True)


def dispatch_kernel(near, halves, at_ref, ids_ref, ints_ref, tok_ref, grad_ref, *outs):
    hot = slot_onehot(ids_ref[...], near, halves, at_ref[5])
    pick = hot.astype(BF16)
    rows = dot(pick, tok_ref[...]).astype(BF16)
    scale = jnp.sum(jnp.where(hot, token_weights(ints_ref[...]), 0.0), axis=1, keepdims=True)
    grads = (scale * dot(pick, grad_ref[...])).astype(BF16)
    size = halves * CAP
    for k, out_ref in enumerate(outs):
        out_ref[0] = rows[k * size : (k + 1) * size]
        out_ref[1] = grads[k * size : (k + 1) * size]


def combine_kernel(near, halves, at_ref, ids_ref, ints_ref, *refs):
    blocks, (out_ref, din_ref) = refs[:near], refs[near:]
    hot = slot_onehot(ids_ref[...], near, halves, at_ref[5])
    pick = hot.astype(BF16)
    tokens = pick.shape[1]
    eye = lax.broadcasted_iota(jnp.int32, (tokens, tokens), 0) == lax.broadcasted_iota(
        jnp.int32, (tokens, tokens), 1
    )
    scale = jnp.sum(jnp.where(eye, token_weights(ints_ref[...]), 0.0), axis=1, keepdims=True)
    rows = jnp.concatenate([ref[0] for ref in blocks], axis=0)
    grads = jnp.concatenate([ref[1] for ref in blocks], axis=0)
    out_ref[...] = (scale * dot(pick, rows, 0, 0)).astype(BF16)
    din_ref[...] = dot(pick, grads, 0, 0).astype(BF16)


def pieces_kernel(at_ref, gate_ref, up_ref, down_ref, pair_ref, last_ref):
    rows = gate_ref.shape[0]
    lanes = down_ref.shape[1]
    shift = lax.rem(at_ref[0], lanes // rows) * rows
    pick = (
        lax.broadcasted_iota(jnp.int32, (rows, lanes), 1)
        == lax.broadcasted_iota(jnp.int32, (rows, lanes), 0) + shift
    ).astype(BF16)
    pair_ref[0] = gate_ref[...]
    pair_ref[1] = up_ref[...]
    last_ref[0] = dot(pick, down_ref[...], 1, 1).astype(BF16)


def row_mask(half, count, halves, width):
    at = lax.broadcasted_iota(jnp.int32, (count, width), 0)
    return lax.div(lax.rem(at, halves * CAP), CAP) == half


def activations(gate, up, keep):
    sig = jax.nn.sigmoid(gate)
    silu = gate * sig
    return jnp.where(keep, silu * up, jnp.zeros_like(gate)).astype(BF16), sig, silu


def input_grads(gate, up, sig, silu, dh, keep):
    zero = jnp.zeros_like(gate)
    dgate = jnp.where(keep, dh * up * sig * (1.0 + gate * (1.0 - sig)), zero).astype(BF16)
    dup = jnp.where(keep, dh * silu, zero).astype(BF16)
    return dgate, dup


def columns(start, size):
    return pl.ds(pl.multiple_of(start, 128), size)


def emit_partials(grads_ref, hidden, x, own_ref, sends):
    parts = len(sends) + 1
    size = grads_ref.shape[1] // parts
    for k in range(parts):
        at = lax.rem(x + k, parts) * size
        part = dot(grads_ref[:, columns(at, size)], hidden, 0, 0)
        if k == 0:
            own_ref[...] = part
        else:
            sends[k - 1][...] = part.astype(BF16)


def near_kernel(halves, near, at_ref, wg_ref, wu_ref, wd_ref, *refs):
    blocks, (rows_ref, grads_ref, out_ref, dx_ref, own_ref) = refs[:near], refs[near : near + 5]
    sends = refs[near + 5 :]
    size = blocks[0].shape[1]
    for k, ref in enumerate(blocks):
        rows_ref[k * size : (k + 1) * size] = ref[0]
        grads_ref[k * size : (k + 1) * size] = ref[1]
    rows, grads = rows_ref[...], grads_ref[...]
    keep = row_mask(at_ref[0], rows.shape[0], halves, wg_ref.shape[1])
    gate, up = dot(rows, wg_ref[...]), dot(rows, wu_ref[...])
    hidden, sig, silu = activations(gate, up, keep)
    emit_partials(grads_ref, hidden, at_ref[1], own_ref, sends)
    dgate, dup = input_grads(gate, up, sig, silu, dot(grads, wd_ref[...], 1, 1), keep)
    out_ref[...] = dot(hidden, wd_ref[...]).astype(BF16)
    dx_ref[...] = (dot(dgate, wg_ref[...], 1, 1) + dot(dup, wu_ref[...], 1, 1)).astype(BF16)


def far_blocks(x, parts, size, refs):
    own, left, right, low, high = refs
    half = size // 2
    across = lax.rem(x + 2, parts) * size
    return (
        (x * size, own, size),
        (lax.rem(x + parts - 1, parts) * size, left, size),
        (lax.rem(x + 1, parts) * size, right, size),
        (across, low, half),
        (across + half, high, half),
    )


def far_first_kernel(halves, at_ref, rows_ref, grads_ref, *refs):
    weights, (gate_ref, up_ref, hidden_ref, own_ref), sends = refs[:5], refs[5:9], refs[9:]
    parts = len(sends) + 1
    size = rows_ref.shape[1] // parts
    gate = up = None
    for start, ref, count in far_blocks(at_ref[1], parts, size, weights):
        part = rows_ref[:, columns(start, count)]
        g, u = dot(part, ref[0]), dot(part, ref[1])
        gate, up = (g, u) if gate is None else (gate + g, up + u)
    keep = row_mask(1 - at_ref[0], rows_ref.shape[0], halves, gate.shape[1])
    hidden, _, _ = activations(gate, up, keep)
    gate_ref[...], up_ref[...], hidden_ref[...] = gate, up, hidden
    emit_partials(grads_ref, hidden, at_ref[1], own_ref, sends)


def far_last_kernel(halves, parts, at_ref, grads_ref, gate_ref, up_ref, hidden_ref, o_ref, d_ref, *refs):
    pairs, downs, outs = refs[:5], refs[5:10], refs[10:]
    size = grads_ref.shape[1] // parts
    x = at_ref[1]
    dh = None
    for start, ref, count in far_blocks(x, parts, size, downs):
        part = dot(grads_ref[:, columns(start, count)], ref[0])
        dh = part if dh is None else dh + part
    gate, up = gate_ref[...], up_ref[...]
    keep = row_mask(1 - at_ref[0], gate.shape[0], halves, gate.shape[1])
    _, sig, silu = activations(gate, up, keep)
    dgate, dup = input_grads(gate, up, sig, silu, dh, keep)
    hidden = hidden_ref[...]
    rows = outs[0].shape[1]
    for (start, down, count), (_, pair, _) in zip(
        far_blocks(x, parts, size, downs), far_blocks(x, parts, size, pairs)
    ):
        cols = columns(start, count)
        out = dot(hidden, down[0], 1, 1).astype(BF16) + o_ref[:, cols]
        dx = dot(dgate, pair[0], 1, 1) + dot(dup, pair[1], 1, 1)
        dx = dx.astype(BF16) + d_ref[:, cols]
        for k, out_ref in enumerate(outs):
            out_ref[0, :, cols] = out[k * rows : (k + 1) * rows]
            out_ref[1, :, cols] = dx[k * rows : (k + 1) * rows]


def order_kernel(quads, at_ref, *refs):
    ins, out_ref = refs[:-1], refs[-1]
    a, b = at_ref[2], at_ref[3]
    near = len(ins)
    depth = ins[0].shape[2]
    for j, ref in enumerate(ins):
        for i in range(quads):
            a_from = lax.rem(a + quads - i, quads)
            b_from = lax.rem(b + near - j, near)
            start = pl.multiple_of((a_from * near + b_from) * depth, depth)
            for k in range(out_ref.shape[0]):
                out_ref[k, pl.ds(start, depth), :] = ref[i, k]


def sum_x_kernel(quads, count, at_ref, *refs):
    near_in, far_in = refs[:count], refs[count : 2 * count]
    own_ref, sends = refs[2 * count], refs[2 * count + 1 :]
    near_count = len(sends) + 1
    depth = own_ref.shape[2]
    half, b = at_ref[0], at_ref[3]
    for group, where in ((near_in, half), (far_in, 1 - half)):
        for j in range(near_count):
            for a in range(quads):
                owner = lax.rem(b + j, near_count)
                at = pl.ds(pl.multiple_of((a * near_count + owner) * depth, depth), depth)
                total = group[0][at, :]
                for ref in group[1:]:
                    total = total + ref[at, :].astype(F32)
                if j == 0:
                    own_ref[where, a] = total
                else:
                    sends[j - 1][where, a] = total.astype(BF16)


def sum_b_kernel(at_ref, *refs):
    count = refs[0].shape[0]
    ins = [ref for ref in refs if ref.shape[0] == count and len(ref.shape) == 3]
    own_ref, sends = refs[len(ins)], refs[len(ins) + 1 :]
    me = at_ref[4]
    for k in range(count):
        to = lax.rem(me + k, count)
        total = ins[0][to]
        for ref in ins[1:]:
            total = total + ref[to].astype(F32)
        if k == 0:
            own_ref[...] = total
        else:
            sends[k - 1][...] = total.astype(BF16)


def sum_last_kernel(*refs):
    total = refs[0][...]
    for ref in refs[1:-1]:
        total = total + ref[...].astype(F32)
    refs[-1][...] = total


def call(kernel, outs, *args, scalar=True, flops=0):
    return raw_call(kernel, outs, *args, scalar=scalar, flops=flops)


def raw_call(kernel, outs, *args, scalar=True, flops=0):
    vmem = pl.BlockSpec(memory_space=pltpu.VMEM)
    smem = pl.BlockSpec(memory_space=pltpu.SMEM)
    size = sum(a.size * a.dtype.itemsize for a in (*args, *outs))
    return pl.pallas_call(
        kernel,
        out_shape=outs,
        in_specs=[smem if scalar and k == 0 else vmem for k in range(len(args))],
        out_specs=tuple(vmem for _ in outs),
        compiler_params=pltpu.CompilerParams(vmem_limit_bytes=60 << 20),
        cost_estimate=pl.CostEstimate(flops=flops, bytes_accessed=size, transcendentals=0),
    )(*args)


def shape(*dims, dtype=BF16):
    return jax.ShapeDtypeStruct(dims, dtype)


def step(tokens, out_grad, expert_ids, combine_ints, w_gate, w_up, w_down):
    count, width = tokens.shape
    inner = w_gate.shape[2]
    halves, quads, nb, nx = (lax.axis_size(name) for name in ("zh", "a", "b", "x"))
    near = lax.axis_size("y") * lax.axis_size("c")
    depth = width // (nx * quads * nb)
    slots = near * halves * CAP
    zh, x, a, b = (lax.axis_index(name).astype(jnp.int32) for name in ("zh", "x", "a", "b"))
    owner = lax.axis_index(("y", "c")).astype(jnp.int32)
    at = jnp.stack([zh, x, a, b, zh * quads + a, owner])
    shard = ((x * quads + a) * nb + b).reshape(1)
    w_gate, w_up, w_down = w_gate[0], w_up[0], w_down[0]

    per = 128 // depth
    pair, last = pl.pallas_call(
        pieces_kernel,
        grid_spec=pltpu.PrefetchScalarGridSpec(
            num_scalar_prefetch=1,
            grid=(1,),
            in_specs=[
                pl.BlockSpec((depth, inner), lambda i, s: (s[0], 0)),
                pl.BlockSpec((depth, inner), lambda i, s: (s[0], 0)),
                pl.BlockSpec((inner, 128), lambda i, s: (0, lax.div(s[0], per))),
            ],
            out_specs=[
                pl.BlockSpec((2, depth, inner), lambda i, s: (0, 0, 0)),
                pl.BlockSpec((1, depth, inner), lambda i, s: (0, 0, 0)),
            ],
        ),
        out_shape=(shape(2, depth, inner), shape(1, depth, inner)),
    )(shard, w_gate, w_up, w_down)

    def cross(v):
        pairs = [
            [
                (h * quads + i, (1 - h) * quads + (i + k) % quads)
                for h in range(halves)
                for i in range(quads)
            ]
            for k in range(quads)
        ]
        parts = []
        for p in pairs:
            parts.append(lax.ppermute(v, ("zh", "a"), p))
        return jnp.stack(parts)

    def shift(v, name, size, k):
        return lax.ppermute(v, name, [(i, (i + k) % size) for i in range(size)])

    def spread(v):
        m = v.shape[1]
        ins = [v] + [shift(v, "b", nb, k) for k in range(1, nb)]
        return call(
            functools.partial(order_kernel, quads),
            (shape(m, width // nx, inner),), at, *ins,
        )[0]

    def around(v):
        half = v.shape[1] // 2
        left = shift(v, "x", nx, 1)
        right = shift(v, "x", nx, nx - 1)
        low = shift(left[:, :half], "x", nx, 1)
        high = shift(right[:, half:], "x", nx, nx - 1)
        return v, left, right, low, high

    spread_pair = spread(cross(pair))
    last, spread_pair = lax.optimization_barrier((last, spread_pair))
    pairs = around(spread_pair)
    downs = around(spread(cross(last)))

    ids = expert_ids.reshape(1, count)
    ints = combine_ints.T
    packet = (shape(2, halves * CAP, width),) * near
    sends = call(
        functools.partial(dispatch_kernel, near, halves),
        packet, at, ids, ints, tokens, out_grad, flops=4 * slots * count * width,
    )
    both = ("y", "c")
    blocks = [shift(v, both, near, k) if k else v for k, v in enumerate(sends)]
    work = 2 * slots * width * inner
    block = width // nx
    partial_shapes = (shape(block, inner, dtype=F32),) + (shape(block, inner),) * (nx - 1)

    def over_x(own, *sends):
        return (own,) + tuple(shift(v, "x", nx, k + 1) for k, v in enumerate(sends))

    rows, grads, near_out, near_dx, *near_parts = call(
        functools.partial(near_kernel, halves, near),
        (shape(slots, width),) * 4 + partial_shapes,
        at, w_gate, w_up, w_down, *blocks, flops=7 * work,
    )
    near_sums = over_x(*near_parts)
    gate, up, hidden, *far_parts = call(
        functools.partial(far_first_kernel, halves),
        (shape(slots, inner, dtype=F32),) * 2 + (shape(slots, inner),) + partial_shapes,
        at, rows, grads, *pairs, flops=3 * work,
    )
    far_sums = over_x(*far_parts)
    results = call(
        functools.partial(far_last_kernel, halves, nx),
        packet,
        at, grads, gate, up, hidden, near_out, near_dx, *pairs, *downs, flops=4 * work,
    )

    own, *sends = call(
        functools.partial(sum_x_kernel, quads, nx),
        (shape(halves, quads, depth, inner, dtype=F32),)
        + (shape(halves, quads, depth, inner),) * (nb - 1),
        at, *near_sums, *far_sums,
    )
    far = halves * quads
    received = [shift(v, "b", nb, k + 1) for k, v in enumerate(sends)]
    own, *sends = call(
        sum_b_kernel,
        (shape(depth, inner, dtype=F32),) + (shape(depth, inner),) * (far - 1),
        at, *(v.reshape(far, depth, inner) for v in (own, *received)),
    )
    received = [shift(v, ("zh", "a"), far, k + 1) for k, v in enumerate(sends)]
    grad = call(sum_last_kernel, (shape(depth, inner, dtype=F32),), own, *received, scalar=False)[0]

    returned = [shift(v, both, near, near - k) if k else v for k, v in enumerate(results)]
    combined, dinput = call(
        functools.partial(combine_kernel, near, halves),
        (shape(count, width),) * 2, at, ids, ints, *returned,
        flops=4 * slots * count * width,
    )
    return combined, dinput, grad.T[None]


def build(mesh, split):
    fine = Mesh(mesh.devices.reshape(split), AXES)
    token = P(AXES, None)
    expert = P(("zh", "y", "c"), None, None)
    return jax.shard_map(
        step,
        mesh=fine,
        in_specs=(token, token, token, token, expert, expert, expert),
        out_specs=(token, token, P(("zh", "y", "c"), None, ("x", "a", "b"))),
        check_vma=False,
    )


def solution(mesh):
    return build(mesh, SPLIT)
```

```python
import functools

import jax
import jax.numpy as jnp
from jax import lax
from jax.experimental import pallas as pl
from jax.experimental.pallas import tpu as pltpu
from jax.sharding import Mesh, PartitionSpec as P


CAP = 12
AXES = ("zh", "y", "c", "x", "a", "b")
SPLIT = (2, 4, 2, 4, 4, 4)
BF16 = jnp.bfloat16
F32 = jnp.float32


def dot(a, b, ca=1, cb=0):
    return lax.dot_general(a, b, (((ca,), (cb,)), ((), ())), preferred_element_type=F32)


def slot_onehot(ids, near, halves, me):
    tokens = ids.shape[1]
    experts = near * halves
    hot = (lax.broadcasted_iota(jnp.int32, (experts, tokens), 0) == ids).astype(F32)
    before = (
        lax.broadcasted_iota(jnp.int32, (tokens, tokens), 0)
        < lax.broadcasted_iota(jnp.int32, (tokens, tokens), 1)
    ).astype(BF16)
    counts = dot(hot.astype(BF16), before)
    rank = jnp.sum(hot * counts, axis=0, keepdims=True).astype(jnp.int32)
    half = sum((ids >= near * k).astype(jnp.int32) for k in range(1, halves))
    owner = ids - near * half
    hops = jnp.where(owner >= me, owner - me, owner - me + near)
    slot = hops * (halves * CAP) + half * CAP + rank
    return lax.broadcasted_iota(jnp.int32, (experts * CAP, tokens), 0) == slot


def token_weights(ints):
    ints = ints.astype(F32)
    return ints[0:1] / jnp.sum(ints, axis=0, keepdims=True)


def dispatch_kernel(near, halves, at_ref, ids_ref, ints_ref, tok_ref, grad_ref, *outs):
    hot = slot_onehot(ids_ref[...], near, halves, at_ref[5])
    pick = hot.astype(BF16)
    rows = dot(pick, tok_ref[...]).astype(BF16)
    scale = jnp.sum(jnp.where(hot, token_weights(ints_ref[...]), 0.0), axis=1, keepdims=True)
    grads = (scale * dot(pick, grad_ref[...])).astype(BF16)
    size = halves * CAP
    for k, out_ref in enumerate(outs):
        out_ref[0] = rows[k * size : (k + 1) * size]
        out_ref[1] = grads[k * size : (k + 1) * size]


def combine_kernel(near, halves, at_ref, ids_ref, ints_ref, *refs):
    blocks, (out_ref, din_ref) = refs[:near], refs[near:]
    hot = slot_onehot(ids_ref[...], near, halves, at_ref[5])
    pick = hot.astype(BF16)
    tokens = pick.shape[1]
    eye = lax.broadcasted_iota(jnp.int32, (tokens, tokens), 0) == lax.broadcasted_iota(
        jnp.int32, (tokens, tokens), 1
    )
    scale = jnp.sum(jnp.where(eye, token_weights(ints_ref[...]), 0.0), axis=1, keepdims=True)
    rows = jnp.concatenate([ref[0] for ref in blocks], axis=0)
    grads = jnp.concatenate([ref[1] for ref in blocks], axis=0)
    out_ref[...] = (scale * dot(pick, rows, 0, 0)).astype(BF16)
    din_ref[...] = dot(pick, grads, 0, 0).astype(BF16)


def pieces_kernel(at_ref, gate_ref, up_ref, down_ref, out_ref):
    rows = gate_ref.shape[0]
    lanes = down_ref.shape[1]
    shift = lax.rem(at_ref[0], lanes // rows) * rows
    pick = (
        lax.broadcasted_iota(jnp.int32, (rows, lanes), 1)
        == lax.broadcasted_iota(jnp.int32, (rows, lanes), 0) + shift
    ).astype(BF16)
    out_ref[0] = gate_ref[...]
    out_ref[1] = up_ref[...]
    out_ref[2] = dot(pick, down_ref[...], 1, 1).astype(BF16)


def row_mask(half, count, halves, width):
    at = lax.broadcasted_iota(jnp.int32, (count, width), 0)
    return lax.div(lax.rem(at, halves * CAP), CAP) == half


def activations(gate, up, keep):
    sig = jax.nn.sigmoid(gate)
    silu = gate * sig
    return jnp.where(keep, silu * up, jnp.zeros_like(gate)).astype(BF16), sig, silu


def input_grads(gate, up, sig, silu, dh, keep):
    zero = jnp.zeros_like(gate)
    dgate = jnp.where(keep, dh * up * sig * (1.0 + gate * (1.0 - sig)), zero).astype(BF16)
    dup = jnp.where(keep, dh * silu, zero).astype(BF16)
    return dgate, dup


def columns(start, size):
    return pl.ds(pl.multiple_of(start, 128), size)


def emit_partials(grads_ref, hidden, x, own_ref, sends):
    parts = len(sends) + 1
    size = grads_ref.shape[1] // parts
    for k in range(parts):
        at = lax.rem(x + k, parts) * size
        part = dot(grads_ref[:, columns(at, size)], hidden, 0, 0)
        if k == 0:
            own_ref[...] = part
        else:
            sends[k - 1][...] = part.astype(BF16)


def near_kernel(halves, near, at_ref, wg_ref, wu_ref, wd_ref, *refs):
    blocks, (rows_ref, grads_ref, out_ref, dx_ref, own_ref) = refs[:near], refs[near : near + 5]
    sends = refs[near + 5 :]
    size = blocks[0].shape[1]
    for k, ref in enumerate(blocks):
        rows_ref[k * size : (k + 1) * size] = ref[0]
        grads_ref[k * size : (k + 1) * size] = ref[1]
    rows, grads = rows_ref[...], grads_ref[...]
    keep = row_mask(at_ref[0], rows.shape[0], halves, wg_ref.shape[1])
    gate, up = dot(rows, wg_ref[...]), dot(rows, wu_ref[...])
    hidden, sig, silu = activations(gate, up, keep)
    emit_partials(grads_ref, hidden, at_ref[1], own_ref, sends)
    dgate, dup = input_grads(gate, up, sig, silu, dot(grads, wd_ref[...], 1, 1), keep)
    out_ref[...] = dot(hidden, wd_ref[...]).astype(BF16)
    dx_ref[...] = (dot(dgate, wg_ref[...], 1, 1) + dot(dup, wu_ref[...], 1, 1)).astype(BF16)


def far_blocks(x, parts, size, refs):
    own, left, right, low, high = refs
    half = size // 2
    across = lax.rem(x + 2, parts) * size
    return (
        (x * size, own, size),
        (lax.rem(x + parts - 1, parts) * size, left, size),
        (lax.rem(x + 1, parts) * size, right, size),
        (across, low, half),
        (across + half, high, half),
    )


def far_first_kernel(halves, at_ref, rows_ref, grads_ref, *refs):
    weights, (gate_ref, up_ref, hidden_ref, own_ref), sends = refs[:5], refs[5:9], refs[9:]
    parts = len(sends) + 1
    size = rows_ref.shape[1] // parts
    gate = up = None
    for start, ref, count in far_blocks(at_ref[1], parts, size, weights):
        part = rows_ref[:, columns(start, count)]
        g, u = dot(part, ref[0]), dot(part, ref[1])
        gate, up = (g, u) if gate is None else (gate + g, up + u)
    keep = row_mask(1 - at_ref[0], rows_ref.shape[0], halves, gate.shape[1])
    hidden, _, _ = activations(gate, up, keep)
    gate_ref[...], up_ref[...], hidden_ref[...] = gate, up, hidden
    emit_partials(grads_ref, hidden, at_ref[1], own_ref, sends)


def far_last_kernel(halves, parts, at_ref, grads_ref, gate_ref, up_ref, hidden_ref, o_ref, d_ref, *refs):
    weights, outs = refs[:5], refs[5:]
    size = grads_ref.shape[1] // parts
    x = at_ref[1]
    dh = None
    for start, ref, count in far_blocks(x, parts, size, weights):
        part = dot(grads_ref[:, columns(start, count)], ref[2])
        dh = part if dh is None else dh + part
    gate, up = gate_ref[...], up_ref[...]
    keep = row_mask(1 - at_ref[0], gate.shape[0], halves, gate.shape[1])
    _, sig, silu = activations(gate, up, keep)
    dgate, dup = input_grads(gate, up, sig, silu, dh, keep)
    hidden = hidden_ref[...]
    rows = outs[0].shape[1]
    for start, ref, count in far_blocks(x, parts, size, weights):
        cols = columns(start, count)
        out = dot(hidden, ref[2], 1, 1).astype(BF16) + o_ref[:, cols]
        dx = dot(dgate, ref[0], 1, 1) + dot(dup, ref[1], 1, 1)
        dx = dx.astype(BF16) + d_ref[:, cols]
        for k, out_ref in enumerate(outs):
            out_ref[0, :, cols] = out[k * rows : (k + 1) * rows]
            out_ref[1, :, cols] = dx[k * rows : (k + 1) * rows]


def order_kernel(quads, at_ref, *refs):
    ins, out_ref = refs[:-1], refs[-1]
    a, b = at_ref[2], at_ref[3]
    near = len(ins)
    depth = ins[0].shape[2]
    for j, ref in enumerate(ins):
        for i in range(quads):
            a_from = lax.rem(a + quads - i, quads)
            b_from = lax.rem(b + near - j, near)
            start = pl.multiple_of((a_from * near + b_from) * depth, depth)
            for k in range(out_ref.shape[0]):
                out_ref[k, pl.ds(start, depth), :] = ref[i, k]


def sum_x_kernel(quads, count, at_ref, *refs):
    near_in, far_in = refs[:count], refs[count : 2 * count]
    own_ref, sends = refs[2 * count], refs[2 * count + 1 :]
    near_count = len(sends) + 1
    depth = own_ref.shape[2]
    half, b = at_ref[0], at_ref[3]
    for group, where in ((near_in, half), (far_in, 1 - half)):
        for j in range(near_count):
            for a in range(quads):
                owner = lax.rem(b + j, near_count)
                at = pl.ds(pl.multiple_of((a * near_count + owner) * depth, depth), depth)
                total = group[0][at, :]
                for ref in group[1:]:
                    total = total + ref[at, :].astype(F32)
                if j == 0:
                    own_ref[where, a] = total
                else:
                    sends[j - 1][where, a] = total.astype(BF16)


def sum_b_kernel(at_ref, first_ref, *refs):
    ins, (own_ref, send_ref) = refs[:-2], refs[-2:]
    me = at_ref[4]
    for k in range(first_ref.shape[0]):
        total = first_ref[k]
        for ref in ins:
            total = total + ref[k].astype(F32)
        send_ref[k] = total.astype(BF16)

    total = first_ref[me]
    for ref in ins:
        total = total + ref[me].astype(F32)
    own_ref[...] = total


def sum_last_kernel(at_ref, own_ref, in_ref, out_ref):
    me = at_ref[4]
    total = own_ref[...]
    for k in range(in_ref.shape[0]):
        part = in_ref[k].astype(F32)
        total = total + jnp.where(me == k, jnp.zeros_like(part), part)
    out_ref[...] = total


def call(kernel, outs, *args, scalar=True, flops=0):
    return raw_call(kernel, outs, *args, scalar=scalar, flops=flops)


def raw_call(kernel, outs, *args, scalar=True, flops=0):
    vmem = pl.BlockSpec(memory_space=pltpu.VMEM)
    smem = pl.BlockSpec(memory_space=pltpu.SMEM)
    size = sum(a.size * a.dtype.itemsize for a in (*args, *outs))
    return pl.pallas_call(
        kernel,
        out_shape=outs,
        in_specs=[smem if scalar and k == 0 else vmem for k in range(len(args))],
        out_specs=tuple(vmem for _ in outs),
        compiler_params=pltpu.CompilerParams(vmem_limit_bytes=60 << 20),
        cost_estimate=pl.CostEstimate(flops=flops, bytes_accessed=size, transcendentals=0),
    )(*args)


def shape(*dims, dtype=BF16):
    return jax.ShapeDtypeStruct(dims, dtype)


def step(tokens, out_grad, expert_ids, combine_ints, w_gate, w_up, w_down):
    count, width = tokens.shape
    inner = w_gate.shape[2]
    halves, quads, nb, nx = (lax.axis_size(name) for name in ("zh", "a", "b", "x"))
    near = lax.axis_size("y") * lax.axis_size("c")
    depth = width // (nx * quads * nb)
    slots = near * halves * CAP
    zh, x, a, b = (lax.axis_index(name).astype(jnp.int32) for name in ("zh", "x", "a", "b"))
    owner = lax.axis_index(("y", "c")).astype(jnp.int32)
    at = jnp.stack([zh, x, a, b, zh * quads + a, owner])
    shard = ((x * quads + a) * nb + b).reshape(1)
    w_gate, w_up, w_down = w_gate[0], w_up[0], w_down[0]

    per = 128 // depth
    piece = pl.pallas_call(
        pieces_kernel,
        grid_spec=pltpu.PrefetchScalarGridSpec(
            num_scalar_prefetch=1,
            grid=(1,),
            in_specs=[
                pl.BlockSpec((depth, inner), lambda i, s: (s[0], 0)),
                pl.BlockSpec((depth, inner), lambda i, s: (s[0], 0)),
                pl.BlockSpec((inner, 128), lambda i, s: (0, lax.div(s[0], per))),
            ],
            out_specs=pl.BlockSpec((3, depth, inner), lambda i, s: (0, 0, 0)),
        ),
        out_shape=shape(3, depth, inner),
    )(shard, w_gate, w_up, w_down)

    def cross(v):
        pairs = [
            [
                (h * quads + i, (1 - h) * quads + (i + k) % quads)
                for h in range(halves)
                for i in range(quads)
            ]
            for k in range(quads)
        ]
        parts = []
        for p in pairs:
            parts.append(lax.ppermute(v, ("zh", "a"), p))
        return jnp.stack(parts)

    def shift(v, name, size, k):
        return lax.ppermute(v, name, [(i, (i + k) % size) for i in range(size)])

    def spread(v):
        m = v.shape[1]
        ins = [v] + [shift(v, "b", nb, k) for k in range(1, nb)]
        return call(
            functools.partial(order_kernel, quads),
            (shape(m, width // nx, inner),), at, *ins,
        )[0]

    def around(v):
        half = v.shape[1] // 2
        left = shift(v, "x", nx, 1)
        right = shift(v, "x", nx, nx - 1)
        low = shift(left[:, :half], "x", nx, 1)
        high = shift(right[:, half:], "x", nx, nx - 1)
        return v, left, right, low, high

    far_weights = around(spread(cross(piece)))

    ids = expert_ids.reshape(1, count)
    ints = combine_ints.T
    packet = (shape(2, halves * CAP, width),) * near
    sends = call(
        functools.partial(dispatch_kernel, near, halves),
        packet, at, ids, ints, tokens, out_grad, flops=4 * slots * count * width,
    )
    both = ("y", "c")
    blocks = [shift(v, both, near, k) if k else v for k, v in enumerate(sends)]
    work = 2 * slots * width * inner
    block = width // nx
    partial_shapes = (shape(block, inner, dtype=F32),) + (shape(block, inner),) * (nx - 1)

    def over_x(own, *sends):
        return (own,) + tuple(shift(v, "x", nx, k + 1) for k, v in enumerate(sends))

    rows, grads, near_out, near_dx, *near_parts = call(
        functools.partial(near_kernel, halves, near),
        (shape(slots, width),) * 4 + partial_shapes,
        at, w_gate, w_up, w_down, *blocks, flops=7 * work,
    )
    near_sums = over_x(*near_parts)
    gate, up, hidden, *far_parts = call(
        functools.partial(far_first_kernel, halves),
        (shape(slots, inner, dtype=F32),) * 2 + (shape(slots, inner),) + partial_shapes,
        at, rows, grads, *far_weights, flops=3 * work,
    )
    far_sums = over_x(*far_parts)
    results = call(
        functools.partial(far_last_kernel, halves, nx),
        packet,
        at, grads, gate, up, hidden, near_out, near_dx, *far_weights, flops=4 * work,
    )

    own, *sends = call(
        functools.partial(sum_x_kernel, quads, nx),
        (shape(halves, quads, depth, inner, dtype=F32),)
        + (shape(halves, quads, depth, inner),) * (nb - 1),
        at, *near_sums, *far_sums,
    )
    far = halves * quads
    received = [shift(v, "b", nb, k + 1) for k, v in enumerate(sends)]
    own, send = call(
        sum_b_kernel,
        (shape(depth, inner, dtype=F32), shape(far, depth, inner)),
        at, *(v.reshape(far, depth, inner) for v in (own, *received)),
    )
    received = lax.all_to_all(send, ("zh", "a"), split_axis=0, concat_axis=0, tiled=True)
    grad = call(sum_last_kernel, (shape(depth, inner, dtype=F32),), at, own, received)[0]

    returned = [shift(v, both, near, near - k) if k else v for k, v in enumerate(results)]
    combined, dinput = call(
        functools.partial(combine_kernel, near, halves),
        (shape(count, width),) * 2, at, ids, ints, *returned,
        flops=4 * slots * count * width,
    )
    return combined, dinput, grad.T[None]


def build(mesh, split):
    fine = Mesh(mesh.devices.reshape(split), AXES)
    token = P(AXES, None)
    expert = P(("zh", "y", "c"), None, None)
    return jax.shard_map(
        step,
        mesh=fine,
        in_specs=(token, token, token, token, expert, expert, expert),
        out_specs=(token, token, P(("zh", "y", "c"), None, ("x", "a", "b"))),
        check_vma=False,
    )


def solution(mesh):
    return build(mesh, SPLIT)
```

```python
import functools

import jax
import jax.numpy as jnp
from jax import lax
from jax.experimental import pallas as pl
from jax.experimental.pallas import tpu as pltpu
from jax.sharding import Mesh, PartitionSpec as P


CAP = 12
AXES = ("zh", "y", "c", "x", "a", "b")
SPLIT = (2, 4, 2, 4, 4, 4)
BF16 = jnp.bfloat16
F32 = jnp.float32


def dot(a, b, ca=1, cb=0):
    return lax.dot_general(a, b, (((ca,), (cb,)), ((), ())), preferred_element_type=F32)


def slot_onehot(ids, near, halves, me):
    tokens = ids.shape[1]
    experts = near * halves
    hot = (lax.broadcasted_iota(jnp.int32, (experts, tokens), 0) == ids).astype(F32)
    before = (
        lax.broadcasted_iota(jnp.int32, (tokens, tokens), 0)
        < lax.broadcasted_iota(jnp.int32, (tokens, tokens), 1)
    ).astype(BF16)
    counts = dot(hot.astype(BF16), before)
    rank = jnp.sum(hot * counts, axis=0, keepdims=True).astype(jnp.int32)
    half = sum((ids >= near * k).astype(jnp.int32) for k in range(1, halves))
    owner = ids - near * half
    hops = jnp.where(owner >= me, owner - me, owner - me + near)
    slot = hops * (halves * CAP) + half * CAP + rank
    return lax.broadcasted_iota(jnp.int32, (experts * CAP, tokens), 0) == slot


def token_weights(ints):
    ints = ints.astype(F32)
    return ints[0:1] / jnp.sum(ints, axis=0, keepdims=True)


def dispatch_kernel(near, halves, at_ref, ids_ref, ints_ref, tok_ref, grad_ref, *outs):
    hot = slot_onehot(ids_ref[...], near, halves, at_ref[5])
    pick = hot.astype(BF16)
    rows = dot(pick, tok_ref[...]).astype(BF16)
    scale = jnp.sum(jnp.where(hot, token_weights(ints_ref[...]), 0.0), axis=1, keepdims=True)
    grads = (scale * dot(pick, grad_ref[...])).astype(BF16)
    size = halves * CAP
    for k, out_ref in enumerate(outs):
        out_ref[0] = rows[k * size : (k + 1) * size]
        out_ref[1] = grads[k * size : (k + 1) * size]


def combine_kernel(near, halves, at_ref, ids_ref, ints_ref, *refs):
    blocks, (out_ref, din_ref) = refs[:near], refs[near:]
    hot = slot_onehot(ids_ref[...], near, halves, at_ref[5])
    pick = hot.astype(BF16)
    tokens = pick.shape[1]
    eye = lax.broadcasted_iota(jnp.int32, (tokens, tokens), 0) == lax.broadcasted_iota(
        jnp.int32, (tokens, tokens), 1
    )
    scale = jnp.sum(jnp.where(eye, token_weights(ints_ref[...]), 0.0), axis=1, keepdims=True)
    rows = jnp.concatenate([ref[0] for ref in blocks], axis=0)
    grads = jnp.concatenate([ref[1] for ref in blocks], axis=0)
    out_ref[...] = (scale * dot(pick, rows, 0, 0)).astype(BF16)
    din_ref[...] = dot(pick, grads, 0, 0).astype(BF16)


def pieces_kernel(at_ref, gate_ref, up_ref, down_ref, out_ref):
    rows = gate_ref.shape[0]
    lanes = down_ref.shape[1]
    shift = lax.rem(at_ref[0], lanes // rows) * rows
    pick = (
        lax.broadcasted_iota(jnp.int32, (rows, lanes), 1)
        == lax.broadcasted_iota(jnp.int32, (rows, lanes), 0) + shift
    ).astype(BF16)
    out_ref[0] = gate_ref[...]
    out_ref[1] = up_ref[...]
    out_ref[2] = dot(pick, down_ref[...], 1, 1).astype(BF16)


def row_mask(half, count, halves, width):
    at = lax.broadcasted_iota(jnp.int32, (count, width), 0)
    return lax.div(lax.rem(at, halves * CAP), CAP) == half


def activations(gate, up, keep):
    sig = jax.nn.sigmoid(gate)
    silu = gate * sig
    return jnp.where(keep, silu * up, jnp.zeros_like(gate)).astype(BF16), sig, silu


def input_grads(gate, up, sig, silu, dh, keep):
    zero = jnp.zeros_like(gate)
    dgate = jnp.where(keep, dh * up * sig * (1.0 + gate * (1.0 - sig)), zero).astype(BF16)
    dup = jnp.where(keep, dh * silu, zero).astype(BF16)
    return dgate, dup


def columns(start, size):
    return pl.ds(pl.multiple_of(start, 128), size)


def emit_partials(grads_ref, hidden, x, own_ref, sends):
    parts = len(sends) + 1
    size = grads_ref.shape[1] // parts
    for k in range(parts):
        at = lax.rem(x + k, parts) * size
        part = dot(grads_ref[:, columns(at, size)], hidden, 0, 0)
        if k == 0:
            own_ref[...] = part
        else:
            sends[k - 1][...] = part.astype(BF16)


def near_kernel(halves, near, at_ref, wg_ref, wu_ref, wd_ref, *refs):
    blocks, (rows_ref, grads_ref, out_ref, dx_ref, own_ref) = refs[:near], refs[near : near + 5]
    sends = refs[near + 5 :]
    size = blocks[0].shape[1]
    for k, ref in enumerate(blocks):
        rows_ref[k * size : (k + 1) * size] = ref[0]
        grads_ref[k * size : (k + 1) * size] = ref[1]
    rows, grads = rows_ref[...], grads_ref[...]
    keep = row_mask(at_ref[0], rows.shape[0], halves, wg_ref.shape[1])
    gate, up = dot(rows, wg_ref[...]), dot(rows, wu_ref[...])
    hidden, sig, silu = activations(gate, up, keep)
    emit_partials(grads_ref, hidden, at_ref[1], own_ref, sends)
    dgate, dup = input_grads(gate, up, sig, silu, dot(grads, wd_ref[...], 1, 1), keep)
    out_ref[...] = dot(hidden, wd_ref[...]).astype(BF16)
    dx_ref[...] = (dot(dgate, wg_ref[...], 1, 1) + dot(dup, wu_ref[...], 1, 1)).astype(BF16)


def far_blocks(x, parts, size, refs):
    own, left, right, low, high = refs
    half = size // 2
    across = lax.rem(x + 2, parts) * size
    return (
        (x * size, own, size),
        (lax.rem(x + parts - 1, parts) * size, left, size),
        (lax.rem(x + 1, parts) * size, right, size),
        (across, low, half),
        (across + half, high, half),
    )


def far_first_kernel(halves, at_ref, rows_ref, grads_ref, *refs):
    weights, (gate_ref, up_ref, hidden_ref, own_ref), sends = refs[:5], refs[5:9], refs[9:]
    parts = len(sends) + 1
    size = rows_ref.shape[1] // parts
    gate = up = None
    for start, ref, count in far_blocks(at_ref[1], parts, size, weights):
        part = rows_ref[:, columns(start, count)]
        g, u = dot(part, ref[0]), dot(part, ref[1])
        gate, up = (g, u) if gate is None else (gate + g, up + u)
    keep = row_mask(1 - at_ref[0], rows_ref.shape[0], halves, gate.shape[1])
    hidden, _, _ = activations(gate, up, keep)
    gate_ref[...], up_ref[...], hidden_ref[...] = gate, up, hidden
    emit_partials(grads_ref, hidden, at_ref[1], own_ref, sends)


def far_last_kernel(halves, parts, at_ref, grads_ref, gate_ref, up_ref, hidden_ref, o_ref, d_ref, *refs):
    pairs, downs, outs = refs[:5], refs[5:10], refs[10:]
    size = grads_ref.shape[1] // parts
    x = at_ref[1]
    dh = None
    for start, ref, count in far_blocks(x, parts, size, downs):
        part = dot(grads_ref[:, columns(start, count)], ref[0])
        dh = part if dh is None else dh + part
    gate, up = gate_ref[...], up_ref[...]
    keep = row_mask(1 - at_ref[0], gate.shape[0], halves, gate.shape[1])
    _, sig, silu = activations(gate, up, keep)
    dgate, dup = input_grads(gate, up, sig, silu, dh, keep)
    hidden = hidden_ref[...]
    rows = outs[0].shape[1]
    for (start, down, count), (_, ref, _) in zip(
        far_blocks(x, parts, size, downs), far_blocks(x, parts, size, pairs)
    ):
        cols = columns(start, count)
        out = dot(hidden, down[0], 1, 1).astype(BF16) + o_ref[:, cols]
        dx = dot(dgate, ref[0], 1, 1) + dot(dup, ref[1], 1, 1)
        dx = dx.astype(BF16) + d_ref[:, cols]
        for k, out_ref in enumerate(outs):
            out_ref[0, :, cols] = out[k * rows : (k + 1) * rows]
            out_ref[1, :, cols] = dx[k * rows : (k + 1) * rows]


def order_kernel(quads, at_ref, *refs):
    ins, out_ref = refs[:-1], refs[-1]
    a, b = at_ref[2], at_ref[3]
    near = len(ins)
    depth = ins[0].shape[2]
    for j, ref in enumerate(ins):
        for i in range(quads):
            a_from = lax.rem(a + quads - i, quads)
            b_from = lax.rem(b + near - j, near)
            start = pl.multiple_of((a_from * near + b_from) * depth, depth)
            for k in range(out_ref.shape[0]):
                out_ref[k, pl.ds(start, depth), :] = ref[i, k]


def sum_x_kernel(quads, count, at_ref, *refs):
    near_in, far_in = refs[:count], refs[count : 2 * count]
    own_ref, sends = refs[2 * count], refs[2 * count + 1 :]
    near_count = len(sends) + 1
    depth = own_ref.shape[2]
    half, b = at_ref[0], at_ref[3]
    for group, where in ((near_in, half), (far_in, 1 - half)):
        for j in range(near_count):
            for a in range(quads):
                owner = lax.rem(b + j, near_count)
                at = pl.ds(pl.multiple_of((a * near_count + owner) * depth, depth), depth)
                total = group[0][at, :]
                for ref in group[1:]:
                    total = total + ref[at, :].astype(F32)
                if j == 0:
                    own_ref[where, a] = total
                else:
                    sends[j - 1][where, a] = total.astype(BF16)


def sum_b_kernel(at_ref, first_ref, *refs):
    ins, (own_ref, send_ref) = refs[:-2], refs[-2:]
    me = at_ref[4]
    for k in range(first_ref.shape[0]):
        total = first_ref[k]
        for ref in ins:
            total = total + ref[k].astype(F32)
        send_ref[k] = total.astype(BF16)

    total = first_ref[me]
    for ref in ins:
        total = total + ref[me].astype(F32)
    own_ref[...] = total


def sum_last_kernel(at_ref, own_ref, in_ref, out_ref):
    me = at_ref[4]
    total = own_ref[...]
    for k in range(in_ref.shape[0]):
        part = in_ref[k].astype(F32)
        total = total + jnp.where(me == k, jnp.zeros_like(part), part)
    out_ref[...] = total


def call(kernel, outs, *args, scalar=True, flops=0):
    return raw_call(kernel, outs, *args, scalar=scalar, flops=flops)


def raw_call(kernel, outs, *args, scalar=True, flops=0):
    vmem = pl.BlockSpec(memory_space=pltpu.VMEM)
    smem = pl.BlockSpec(memory_space=pltpu.SMEM)
    size = sum(a.size * a.dtype.itemsize for a in (*args, *outs))
    return pl.pallas_call(
        kernel,
        out_shape=outs,
        in_specs=[smem if scalar and k == 0 else vmem for k in range(len(args))],
        out_specs=tuple(vmem for _ in outs),
        compiler_params=pltpu.CompilerParams(vmem_limit_bytes=60 << 20),
        cost_estimate=pl.CostEstimate(flops=flops, bytes_accessed=size, transcendentals=0),
    )(*args)


def shape(*dims, dtype=BF16):
    return jax.ShapeDtypeStruct(dims, dtype)


def step(tokens, out_grad, expert_ids, combine_ints, w_gate, w_up, w_down):
    count, width = tokens.shape
    inner = w_gate.shape[2]
    halves, quads, nb, nx = (lax.axis_size(name) for name in ("zh", "a", "b", "x"))
    near = lax.axis_size("y") * lax.axis_size("c")
    depth = width // (nx * quads * nb)
    slots = near * halves * CAP
    zh, x, a, b = (lax.axis_index(name).astype(jnp.int32) for name in ("zh", "x", "a", "b"))
    owner = lax.axis_index(("y", "c")).astype(jnp.int32)
    at = jnp.stack([zh, x, a, b, zh * quads + a, owner])
    shard = ((x * quads + a) * nb + b).reshape(1)
    w_gate, w_up, w_down = w_gate[0], w_up[0], w_down[0]

    per = 128 // depth
    piece = pl.pallas_call(
        pieces_kernel,
        grid_spec=pltpu.PrefetchScalarGridSpec(
            num_scalar_prefetch=1,
            grid=(1,),
            in_specs=[
                pl.BlockSpec((depth, inner), lambda i, s: (s[0], 0)),
                pl.BlockSpec((depth, inner), lambda i, s: (s[0], 0)),
                pl.BlockSpec((inner, 128), lambda i, s: (0, lax.div(s[0], per))),
            ],
            out_specs=pl.BlockSpec((3, depth, inner), lambda i, s: (0, 0, 0)),
        ),
        out_shape=shape(3, depth, inner),
    )(shard, w_gate, w_up, w_down)

    def cross(v):
        pairs = [
            [
                (h * quads + i, (1 - h) * quads + (i + k) % quads)
                for h in range(halves)
                for i in range(quads)
            ]
            for k in range(quads)
        ]
        parts = []
        for p in pairs:
            parts.append(lax.ppermute(v, ("zh", "a"), p))
        return parts

    def shift(v, name, size, k):
        return lax.ppermute(v, name, [(i, (i + k) % size) for i in range(size)])

    def spread(v):
        m = v.shape[1]
        ins = [v] + [shift(v, "b", nb, k) for k in range(1, nb)]
        return call(
            functools.partial(order_kernel, quads),
            (shape(m, width // nx, inner),), at, *ins,
        )[0]

    def around(v):
        half = v.shape[1] // 2
        left = shift(v, "x", nx, 1)
        right = shift(v, "x", nx, nx - 1)
        low = shift(left[:, :half], "x", nx, 1)
        high = shift(right[:, half:], "x", nx, nx - 1)
        return v, left, right, low, high

    crossed = lax.optimization_barrier(jnp.stack(cross(piece)))
    pairs = around(spread(crossed[:, :2]))
    downs = around(spread(crossed[:, 2:]))

    ids = expert_ids.reshape(1, count)
    ints = combine_ints.T
    packet = (shape(2, halves * CAP, width),) * near
    sends = call(
        functools.partial(dispatch_kernel, near, halves),
        packet, at, ids, ints, tokens, out_grad, flops=4 * slots * count * width,
    )
    both = ("y", "c")
    blocks = [shift(v, both, near, k) if k else v for k, v in enumerate(sends)]
    work = 2 * slots * width * inner
    block = width // nx
    partial_shapes = (shape(block, inner, dtype=F32),) + (shape(block, inner),) * (nx - 1)

    def over_x(own, *sends):
        return (own,) + tuple(shift(v, "x", nx, k + 1) for k, v in enumerate(sends))

    rows, grads, near_out, near_dx, *near_parts = call(
        functools.partial(near_kernel, halves, near),
        (shape(slots, width),) * 4 + partial_shapes,
        at, w_gate, w_up, w_down, *blocks, flops=7 * work,
    )
    near_sums = over_x(*near_parts)
    gate, up, hidden, *far_parts = call(
        functools.partial(far_first_kernel, halves),
        (shape(slots, inner, dtype=F32),) * 2 + (shape(slots, inner),) + partial_shapes,
        at, rows, grads, *pairs, flops=3 * work,
    )
    far_sums = over_x(*far_parts)
    results = call(
        functools.partial(far_last_kernel, halves, nx),
        packet,
        at, grads, gate, up, hidden, near_out, near_dx, *pairs, *downs, flops=4 * work,
    )

    own, *sends = call(
        functools.partial(sum_x_kernel, quads, nx),
        (shape(halves, quads, depth, inner, dtype=F32),)
        + (shape(halves, quads, depth, inner),) * (nb - 1),
        at, *near_sums, *far_sums,
    )
    far = halves * quads
    received = [shift(v, "b", nb, k + 1) for k, v in enumerate(sends)]
    own, send = call(
        sum_b_kernel,
        (shape(depth, inner, dtype=F32), shape(far, depth, inner)),
        at, *(v.reshape(far, depth, inner) for v in (own, *received)),
    )
    received = lax.all_to_all(send, ("zh", "a"), split_axis=0, concat_axis=0, tiled=True)
    grad = call(sum_last_kernel, (shape(depth, inner, dtype=F32),), at, own, received)[0]

    returned = [shift(v, both, near, near - k) if k else v for k, v in enumerate(results)]
    combined, dinput = call(
        functools.partial(combine_kernel, near, halves),
        (shape(count, width),) * 2, at, ids, ints, *returned,
        flops=4 * slots * count * width,
    )
    return combined, dinput, grad.T[None]


def build(mesh, split):
    fine = Mesh(mesh.devices.reshape(split), AXES)
    token = P(AXES, None)
    expert = P(("zh", "y", "c"), None, None)
    return jax.shard_map(
        step,
        mesh=fine,
        in_specs=(token, token, token, token, expert, expert, expert),
        out_specs=(token, token, P(("zh", "y", "c"), None, ("x", "a", "b"))),
        check_vma=False,
    )


def solution(mesh):
    return build(mesh, SPLIT)
```

```python
import functools

import jax
import jax.numpy as jnp
from jax import lax
from jax.experimental import pallas as pl
from jax.experimental.pallas import tpu as pltpu
from jax.sharding import Mesh, PartitionSpec as P


CAP = 12
AXES = ("zh", "y", "c", "x", "a", "b")
SPLIT = (2, 4, 2, 4, 4, 4)
BF16 = jnp.bfloat16
F32 = jnp.float32


def dot(a, b, ca=1, cb=0):
    return lax.dot_general(a, b, (((ca,), (cb,)), ((), ())), preferred_element_type=F32)


def slot_onehot(ids, near, halves, me):
    tokens = ids.shape[1]
    experts = near * halves
    hot = (lax.broadcasted_iota(jnp.int32, (experts, tokens), 0) == ids).astype(F32)
    before = (
        lax.broadcasted_iota(jnp.int32, (tokens, tokens), 0)
        < lax.broadcasted_iota(jnp.int32, (tokens, tokens), 1)
    ).astype(BF16)
    counts = dot(hot.astype(BF16), before)
    rank = jnp.sum(hot * counts, axis=0, keepdims=True).astype(jnp.int32)
    half = sum((ids >= near * k).astype(jnp.int32) for k in range(1, halves))
    owner = ids - near * half
    hops = jnp.where(owner >= me, owner - me, owner - me + near)
    slot = hops * (halves * CAP) + half * CAP + rank
    return lax.broadcasted_iota(jnp.int32, (experts * CAP, tokens), 0) == slot


def token_weights(ints):
    ints = ints.astype(F32)
    return ints[0:1] / jnp.sum(ints, axis=0, keepdims=True)


def dispatch_kernel(near, halves, at_ref, ids_ref, ints_ref, tok_ref, grad_ref, *outs):
    hot = slot_onehot(ids_ref[...], near, halves, at_ref[5])
    pick = hot.astype(BF16)
    rows = dot(pick, tok_ref[...]).astype(BF16)
    scale = jnp.sum(jnp.where(hot, token_weights(ints_ref[...]), 0.0), axis=1, keepdims=True)
    grads = (scale * dot(pick, grad_ref[...])).astype(BF16)
    size = halves * CAP
    for k, out_ref in enumerate(outs):
        out_ref[0] = rows[k * size : (k + 1) * size]
        out_ref[1] = grads[k * size : (k + 1) * size]


def combine_kernel(near, halves, at_ref, ids_ref, ints_ref, *refs):
    blocks, (out_ref, din_ref) = refs[:near], refs[near:]
    hot = slot_onehot(ids_ref[...], near, halves, at_ref[5])
    pick = hot.astype(BF16)
    tokens = pick.shape[1]
    eye = lax.broadcasted_iota(jnp.int32, (tokens, tokens), 0) == lax.broadcasted_iota(
        jnp.int32, (tokens, tokens), 1
    )
    scale = jnp.sum(jnp.where(eye, token_weights(ints_ref[...]), 0.0), axis=1, keepdims=True)
    rows = jnp.concatenate([ref[0] for ref in blocks], axis=0)
    grads = jnp.concatenate([ref[1] for ref in blocks], axis=0)
    out_ref[...] = (scale * dot(pick, rows, 0, 0)).astype(BF16)
    din_ref[...] = dot(pick, grads, 0, 0).astype(BF16)


def pieces_kernel(at_ref, *refs):
    ins, (own_ref, out_ref) = refs[:-2], refs[-2:]
    for k in range(2):
        gate_ref, up_ref, down_ref = ins[3 * k : 3 * k + 3]
        rows = gate_ref.shape[0]
        lanes = down_ref.shape[1]
        shift = lax.rem(at_ref[k], lanes // rows) * rows
        pick = (
            lax.broadcasted_iota(jnp.int32, (rows, lanes), 1)
            == lax.broadcasted_iota(jnp.int32, (rows, lanes), 0) + shift
        ).astype(BF16)
        out_ref[k, 0] = gate_ref[...]
        out_ref[k, 1] = up_ref[...]
        out_ref[k, 2] = dot(pick, down_ref[...], 1, 1).astype(BF16)
    own_ref[...] = out_ref[0]


def row_mask(half, count, halves, width):
    at = lax.broadcasted_iota(jnp.int32, (count, width), 0)
    return lax.div(lax.rem(at, halves * CAP), CAP) == half


def activations(gate, up, keep):
    sig = jax.nn.sigmoid(gate)
    silu = gate * sig
    return jnp.where(keep, silu * up, jnp.zeros_like(gate)).astype(BF16), sig, silu


def input_grads(gate, up, sig, silu, dh, keep):
    zero = jnp.zeros_like(gate)
    dgate = jnp.where(keep, dh * up * sig * (1.0 + gate * (1.0 - sig)), zero).astype(BF16)
    dup = jnp.where(keep, dh * silu, zero).astype(BF16)
    return dgate, dup


def columns(start, size):
    return pl.ds(pl.multiple_of(start, 128), size)


def emit_partials(grads_ref, hidden, x, own_ref, sends):
    parts = len(sends) + 1
    size = grads_ref.shape[1] // parts
    for k in range(parts):
        at = lax.rem(x + k, parts) * size
        part = dot(grads_ref[:, columns(at, size)], hidden, 0, 0)
        if k == 0:
            own_ref[...] = part
        else:
            sends[k - 1][...] = part.astype(BF16)


def near_kernel(halves, near, at_ref, wg_ref, wu_ref, wd_ref, *refs):
    blocks, (rows_ref, grads_ref, out_ref, dx_ref, own_ref) = refs[:near], refs[near : near + 5]
    sends = refs[near + 5 :]
    size = blocks[0].shape[1]
    for k, ref in enumerate(blocks):
        rows_ref[k * size : (k + 1) * size] = ref[0]
        grads_ref[k * size : (k + 1) * size] = ref[1]
    rows, grads = rows_ref[...], grads_ref[...]
    keep = row_mask(at_ref[0], rows.shape[0], halves, wg_ref.shape[1])
    gate, up = dot(rows, wg_ref[...]), dot(rows, wu_ref[...])
    hidden, sig, silu = activations(gate, up, keep)
    emit_partials(grads_ref, hidden, at_ref[1], own_ref, sends)
    dgate, dup = input_grads(gate, up, sig, silu, dot(grads, wd_ref[...], 1, 1), keep)
    out_ref[...] = dot(hidden, wd_ref[...]).astype(BF16)
    dx_ref[...] = (dot(dgate, wg_ref[...], 1, 1) + dot(dup, wu_ref[...], 1, 1)).astype(BF16)


def far_blocks(x, parts, size, refs):
    own, left, right, low, high = refs
    half = size // 2
    across = lax.rem(x + 2, parts) * size
    return (
        (x * size, own, size),
        (lax.rem(x + parts - 1, parts) * size, left, size),
        (lax.rem(x + 1, parts) * size, right, size),
        (across, low, half),
        (across + half, high, half),
    )


def far_first_kernel(halves, at_ref, rows_ref, grads_ref, *refs):
    weights, (gate_ref, up_ref, hidden_ref, own_ref), sends = refs[:5], refs[5:9], refs[9:]
    parts = len(sends) + 1
    size = rows_ref.shape[1] // parts
    gate = up = None
    for start, ref, count in far_blocks(at_ref[1], parts, size, weights):
        part = rows_ref[:, columns(start, count)]
        g, u = dot(part, ref[0]), dot(part, ref[1])
        gate, up = (g, u) if gate is None else (gate + g, up + u)
    keep = row_mask(1 - at_ref[0], rows_ref.shape[0], halves, gate.shape[1])
    hidden, _, _ = activations(gate, up, keep)
    gate_ref[...], up_ref[...], hidden_ref[...] = gate, up, hidden
    emit_partials(grads_ref, hidden, at_ref[1], own_ref, sends)


def far_last_kernel(halves, parts, at_ref, grads_ref, gate_ref, up_ref, hidden_ref, o_ref, d_ref, *refs):
    pairs, downs, outs = refs[:5], refs[5:10], refs[10:]
    size = grads_ref.shape[1] // parts
    x = at_ref[1]
    dh = None
    for start, ref, count in far_blocks(x, parts, size, downs):
        part = dot(grads_ref[:, columns(start, count)], ref[0])
        dh = part if dh is None else dh + part
    gate, up = gate_ref[...], up_ref[...]
    keep = row_mask(1 - at_ref[0], gate.shape[0], halves, gate.shape[1])
    _, sig, silu = activations(gate, up, keep)
    dgate, dup = input_grads(gate, up, sig, silu, dh, keep)
    hidden = hidden_ref[...]
    rows = outs[0].shape[1]
    for (start, down, count), (_, ref, _) in zip(
        far_blocks(x, parts, size, downs), far_blocks(x, parts, size, pairs)
    ):
        cols = columns(start, count)
        out = dot(hidden, down[0], 1, 1).astype(BF16) + o_ref[:, cols]
        dx = dot(dgate, ref[0], 1, 1) + dot(dup, ref[1], 1, 1)
        dx = dx.astype(BF16) + d_ref[:, cols]
        for k, out_ref in enumerate(outs):
            out_ref[0, :, cols] = out[k * rows : (k + 1) * rows]
            out_ref[1, :, cols] = dx[k * rows : (k + 1) * rows]


def order_kernel(quads, at_ref, *refs):
    ins, out_ref = refs[:-1], refs[-1]
    a, b = at_ref[2], at_ref[3]
    near = len(ins)
    depth = ins[0].shape[2]
    for j, ref in enumerate(ins):
        for i in range(quads):
            a_from = lax.rem(a + quads - i, quads)
            b_from = lax.rem(b + near - j, near)
            start = pl.multiple_of((a_from * near + b_from) * depth, depth)
            for k in range(out_ref.shape[0]):
                out_ref[k, pl.ds(start, depth), :] = ref[i, k]


def sum_x_kernel(quads, count, at_ref, *refs):
    near_in, far_in = refs[:count], refs[count : 2 * count]
    own_ref, sends = refs[2 * count], refs[2 * count + 1 :]
    near_count = len(sends) + 1
    depth = own_ref.shape[2]
    half, b = at_ref[0], at_ref[3]
    for group, where in ((near_in, half), (far_in, 1 - half)):
        for j in range(near_count):
            for a in range(quads):
                owner = lax.rem(b + j, near_count)
                at = pl.ds(pl.multiple_of((a * near_count + owner) * depth, depth), depth)
                total = group[0][at, :]
                for ref in group[1:]:
                    total = total + ref[at, :].astype(F32)
                if j == 0:
                    own_ref[where, a] = total
                else:
                    sends[j - 1][where, a] = total.astype(BF16)


def sum_b_kernel(at_ref, first_ref, *refs):
    ins, (own_ref, send_ref) = refs[:-2], refs[-2:]
    me = at_ref[4]
    for k in range(first_ref.shape[0]):
        total = first_ref[k]
        for ref in ins:
            total = total + ref[k].astype(F32)
        send_ref[k] = total.astype(BF16)

    total = first_ref[me]
    for ref in ins:
        total = total + ref[me].astype(F32)
    own_ref[...] = total


def sum_last_kernel(at_ref, own_ref, in_ref, out_ref):
    me = at_ref[4]
    total = own_ref[...]
    for k in range(in_ref.shape[0]):
        part = in_ref[k].astype(F32)
        total = total + jnp.where(me == k, jnp.zeros_like(part), part)
    out_ref[...] = total


def call(kernel, outs, *args, scalar=True, flops=0):
    return raw_call(kernel, outs, *args, scalar=scalar, flops=flops)


def raw_call(kernel, outs, *args, scalar=True, flops=0):
    vmem = pl.BlockSpec(memory_space=pltpu.VMEM)
    smem = pl.BlockSpec(memory_space=pltpu.SMEM)
    size = sum(a.size * a.dtype.itemsize for a in (*args, *outs))
    return pl.pallas_call(
        kernel,
        out_shape=outs,
        in_specs=[smem if scalar and k == 0 else vmem for k in range(len(args))],
        out_specs=tuple(vmem for _ in outs),
        compiler_params=pltpu.CompilerParams(vmem_limit_bytes=60 << 20),
        cost_estimate=pl.CostEstimate(flops=flops, bytes_accessed=size, transcendentals=0),
    )(*args)


def shape(*dims, dtype=BF16):
    return jax.ShapeDtypeStruct(dims, dtype)


def step(tokens, out_grad, expert_ids, combine_ints, w_gate, w_up, w_down):
    count, width = tokens.shape
    inner = w_gate.shape[2]
    halves, quads, nb, nx = (lax.axis_size(name) for name in ("zh", "a", "b", "x"))
    near = lax.axis_size("y") * lax.axis_size("c")
    depth = width // (nx * quads * nb)
    slots = near * halves * CAP
    zh, x, a, b = (lax.axis_index(name).astype(jnp.int32) for name in ("zh", "x", "a", "b"))
    owner = lax.axis_index(("y", "c")).astype(jnp.int32)
    at = jnp.stack([zh, x, a, b, zh * quads + a, owner])
    away = jnp.where(a >= quads // 2, a - quads // 2, a + quads // 2)
    shard = jnp.stack([(x * quads + quad) * nb + b for quad in (a, away)])
    w_gate, w_up, w_down = w_gate[0], w_up[0], w_down[0]

    per = 128 // depth
    piece, pieces = pl.pallas_call(
        pieces_kernel,
        grid_spec=pltpu.PrefetchScalarGridSpec(
            num_scalar_prefetch=1,
            grid=(1,),
            in_specs=[
                spec
                for k in range(2)
                for spec in (
                    pl.BlockSpec((depth, inner), lambda i, s, k=k: (s[k], 0)),
                    pl.BlockSpec((depth, inner), lambda i, s, k=k: (s[k], 0)),
                    pl.BlockSpec((inner, 128), lambda i, s, k=k: (0, lax.div(s[k], per))),
                )
            ],
            out_specs=[
                pl.BlockSpec((3, depth, inner), lambda i, s: (0, 0, 0)),
                pl.BlockSpec((2, 3, depth, inner), lambda i, s: (0, 0, 0, 0)),
            ],
        ),
        out_shape=(shape(3, depth, inner), shape(2, 3, depth, inner)),
    )(shard, *((w_gate, w_up, w_down) * 2))

    def cross(own, two):
        def hop(u, k):
            pairs = [
                (h * quads + i, (1 - h) * quads + (i + k) % quads)
                for h in range(halves)
                for i in range(quads)
            ]
            return lax.ppermute(u, ("zh", "a"), pairs)

        one, both, three = hop(own, 1), hop(two, 2), hop(own, 3)
        return jnp.stack([both[1], one, both[0], three])

    def shift(v, name, size, k):
        return lax.ppermute(v, name, [(i, (i + k) % size) for i in range(size)])

    def spread(v):
        m = v.shape[1]
        ins = [v] + [shift(v, "b", nb, k) for k in range(1, nb)]
        return call(
            functools.partial(order_kernel, quads),
            (shape(m, width // nx, inner),), at, *ins,
        )[0]

    def around(v):
        half = v.shape[1] // 2
        left = shift(v, "x", nx, 1)
        right = shift(v, "x", nx, nx - 1)
        low = shift(left[:, :half], "x", nx, 1)
        high = shift(right[:, half:], "x", nx, nx - 1)
        return v, left, right, low, high

    crossed = lax.optimization_barrier(cross(piece, pieces))
    pairs = around(spread(crossed[:, :2]))
    downs = around(spread(crossed[:, 2:]))

    ids = expert_ids.reshape(1, count)
    ints = combine_ints.T
    packet = (shape(2, halves * CAP, width),) * near
    sends = call(
        functools.partial(dispatch_kernel, near, halves),
        packet, at, ids, ints, tokens, out_grad, flops=4 * slots * count * width,
    )
    both = ("y", "c")
    blocks = [shift(v, both, near, k) if k else v for k, v in enumerate(sends)]
    work = 2 * slots * width * inner
    block = width // nx
    partial_shapes = (shape(block, inner, dtype=F32),) + (shape(block, inner),) * (nx - 1)

    def over_x(own, *sends):
        return (own,) + tuple(shift(v, "x", nx, k + 1) for k, v in enumerate(sends))

    rows, grads, near_out, near_dx, *near_parts = call(
        functools.partial(near_kernel, halves, near),
        (shape(slots, width),) * 4 + partial_shapes,
        at, w_gate, w_up, w_down, *blocks, flops=7 * work,
    )
    near_sums = over_x(*near_parts)
    gate, up, hidden, *far_parts = call(
        functools.partial(far_first_kernel, halves),
        (shape(slots, inner, dtype=F32),) * 2 + (shape(slots, inner),) + partial_shapes,
        at, rows, grads, *pairs, flops=3 * work,
    )
    far_sums = over_x(*far_parts)
    results = call(
        functools.partial(far_last_kernel, halves, nx),
        packet,
        at, grads, gate, up, hidden, near_out, near_dx, *pairs, *downs, flops=4 * work,
    )

    own, *sends = call(
        functools.partial(sum_x_kernel, quads, nx),
        (shape(halves, quads, depth, inner, dtype=F32),)
        + (shape(halves, quads, depth, inner),) * (nb - 1),
        at, *near_sums, *far_sums,
    )
    far = halves * quads
    received = [shift(v, "b", nb, k + 1) for k, v in enumerate(sends)]
    own, send = call(
        sum_b_kernel,
        (shape(depth, inner, dtype=F32), shape(far, depth, inner)),
        at, *(v.reshape(far, depth, inner) for v in (own, *received)),
    )
    received = lax.all_to_all(send, ("zh", "a"), split_axis=0, concat_axis=0, tiled=True)
    grad = call(sum_last_kernel, (shape(depth, inner, dtype=F32),), at, own, received)[0]

    returned = [shift(v, both, near, near - k) if k else v for k, v in enumerate(results)]
    combined, dinput = call(
        functools.partial(combine_kernel, near, halves),
        (shape(count, width),) * 2, at, ids, ints, *returned,
        flops=4 * slots * count * width,
    )
    return combined, dinput, grad.T[None]


def build(mesh, split):
    fine = Mesh(mesh.devices.reshape(split), AXES)
    token = P(AXES, None)
    expert = P(("zh", "y", "c"), None, None)
    return jax.shard_map(
        step,
        mesh=fine,
        in_specs=(token, token, token, token, expert, expert, expert),
        out_specs=(token, token, P(("zh", "y", "c"), None, ("x", "a", "b"))),
        check_vma=False,
    )


def solution(mesh):
    return build(mesh, SPLIT)
```
